32 devices in a mesh: tm: 16 (over z, y, x), col: 2 (over core).
Axes of the slice: x: 2, y: 2, z: 4, core: 2. Of those that a mesh axis runs over, the one named last changes fastest.
Arguments:
- rhs: float32 [16, 1024, 256], P('tm', 'col'), may hold values from -6 to 6
- inverse_blocks: float32 [3, 16, 1024, 1024], P(None, 'tm', None, 'col'), may hold values from -2 to 3, as said below
- lower_coupling: float32 [3, 16, 1024, 1024], P(None, 'tm', None, 'col'), may hold values from -0.1875 to 0.1875
- upper_coupling: float32 [3, 16, 1024, 1024], P(None, 'tm', None, 'col'), may hold values from -0.1875 to 0.1875
- tile_pattern: int32 [3, 16, 2, 8, 8], P(None, 'tm', None, None, 'col'), may hold values from 0 to 1, as said below
- tip_coupling: float32 [3, 16, 64, 1024], P(None, 'tm', None, 'col'), may hold values from -0.046875 to 0.046875
- tip_rhs: float32 [64, 256], replicated, may hold values from -6 to 6
Outputs:
- reduced: float32 [16, 1024, 256], P('tm', 'col')
- tip_reduced: float32 [64, 256], replicated
The draws below stay inside these ranges and needn't reach their ends.
Inputs may be any that keep to these rules, and one draw needn't show every extreme that they name: Every inverse_blocks[l, j] is symmetric. tile_pattern[l, j, k, r, c] is 1 exactly where |r - c| is at most a half-width w[l, j, k] of 1 to 4; both half-widths 1 and 4 occur.
All inputs are finite; a program needn't handle non-finite values.
Results may differ from the reference program's by a relative error of at most 0.0001.
Values sent between devices are 32-bit elements; how exact they have to be, the bound alone decides.
A program may use at most 64 MiB of HBM per device.

```python
import math
import jax
import jax.numpy as jnp
from jax import lax

B = 1024
F = 64
NT = 8
REDUCTION_DEPTH = 3
R = 256
NB = 16


def draw_inverse_blocks(key, part):
    noise_draw = jnp.clip(jax.random.normal(key, (REDUCTION_DEPTH, NB, B, B), jnp.float32), -6.0, 6.0)
    symmetric = (noise_draw + jnp.swapaxes(noise_draw, 2, 3)) * (0.1 / math.sqrt(2.0 * B))
    diagonal = jnp.exp(jax.random.uniform(jax.random.fold_in(key, 1), (REDUCTION_DEPTH, NB, B), jnp.float32, math.log(0.25), math.log(0.5)))
    blocks = symmetric + diagonal[:, :, :, None] * jnp.eye(B, dtype=jnp.float32)[None, None]
    return blocks


def draw_tile_pattern(key, part):
    widest = NT // 2
    band_width = jax.random.randint(key, (REDUCTION_DEPTH, NB, 2), 1, widest + 1)
    band_width = band_width.at[0, 0, 0].set(1).at[0, 0, 1].set(widest)
    tile_index = jnp.arange(NT)
    tile_gap = jnp.abs(tile_index[:, None] - tile_index[None, :])
    return (tile_gap[None, None, None] <= band_width[:, :, :, None, None]).astype(jnp.int32)


def levels(rng, dims, cuts, least, largest):
    level, own = 1.0, jax.random.fold_in(rng, 6)
    for position, blocks in cuts:
        steps = jnp.exp(jax.random.uniform(jax.random.fold_in(own, position), (blocks,), jnp.float32, least / len(cuts), largest / len(cuts)))
        level = level * jnp.repeat(steps, dims[position] // blocks).reshape([-1 if axis == position else 1 for axis in range(len(dims))])
    return level


def normal_values(own_key, extent, deviation, bound, shards=(), kind=jnp.bfloat16):
    level = levels(own_key, extent, shards, -0.22, 0.18) if shards else 1.0
    drawn = jax.random.normal(own_key, extent, jnp.float32) * deviation * level
    return jnp.minimum(jnp.maximum(drawn, -bound), bound).astype(kind)


def setup_inputs(seed: int = 0) -> dict:
    key_of = jax.random.split(jax.random.key(seed), 8)
    rhs = normal_values(key_of[0], (NB, B, R), 1.0, 6.0, ((0, 16), (1, 2)), jnp.float32)
    inverse_blocks = draw_inverse_blocks(jax.random.fold_in(key_of[7], 71), 0)
    lower_coupling = normal_values(key_of[2], (REDUCTION_DEPTH, NB, B, B), B ** -0.5, 0.1875, ((1, 16), (3, 2)), jnp.float32)
    upper_coupling = normal_values(key_of[3], (REDUCTION_DEPTH, NB, B, B), B ** -0.5, 0.1875, ((1, 16), (3, 2)), jnp.float32)
    tile_pattern = draw_tile_pattern(jax.random.fold_in(key_of[7], 71), 0)
    tip_coupling = normal_values(key_of[5], (REDUCTION_DEPTH, NB, F, B), (B * NB) ** -0.5, 0.046875, ((1, 16), (3, 2)), jnp.float32)
    tip_rhs = normal_values(key_of[6], (F, R), 1.0, 6.0, (), jnp.float32)
    return {"rhs": rhs, "inverse_blocks": inverse_blocks, "lower_coupling": lower_coupling, "upper_coupling": upper_coupling, "tile_pattern": tile_pattern, "tip_coupling": tip_coupling, "tip_rhs": tip_rhs}


def expand(pattern):
    tile_size = B // NT
    widened = jnp.repeat(pattern.astype(jnp.float32), tile_size, axis=1)
    return jnp.repeat(widened, tile_size, axis=2)


def reference(rhs, inverse_blocks, lower_coupling, upper_coupling, tile_pattern, tip_coupling, tip_rhs):
    highest = lax.Precision.HIGHEST
    present_rows = rhs
    tip_total = tip_rhs
    for level_number in range(REDUCTION_DEPTH):
        stride = 2 ** level_number
        lower_masked = lower_coupling[level_number] * expand(tile_pattern[level_number, :, 0])
        upper_masked = upper_coupling[level_number] * expand(tile_pattern[level_number, :, 1])
        solved = jnp.einsum("jab,jbr->jar", inverse_blocks[level_number], present_rows, precision=highest)
        down_term = jnp.einsum("jba,jbr->jar", lower_masked, solved, precision=highest)
        up_term = jnp.einsum("jba,jbr->jar", upper_masked, solved, precision=highest)
        present_rows = present_rows - jnp.roll(down_term, -stride, axis=0) - jnp.roll(up_term, stride, axis=0)
        tip_total = tip_total - jnp.einsum("jfb,jbr->fr", tip_coupling[level_number], solved, precision=highest)
    return present_rows, tip_total
```

```python
import functools

import jax
import jax.numpy as jnp
from jax import lax
from jax.experimental import pallas as pl
from jax.experimental.pallas import tpu as pltpu
from jax.sharding import PartitionSpec as P

MESH = pl.DeviceIdType.MESH
LANES = 128
ROWS = 8


def halves_of(x):
    high = x.astype(jnp.bfloat16)
    low = (x - high.astype(jnp.float32)).astype(jnp.bfloat16)
    return high, low


def product(stacked, high, w_high, w_low):
    rows = high.shape[0]
    both = jnp.dot(stacked, w_high, preferred_element_type=jnp.float32)
    return both[:rows] + both[rows:] + jnp.dot(high, w_low, preferred_element_type=jnp.float32)


def kernel(
    dims,
    rhs_hbm,
    inv_hbm,
    low_hbm,
    up_hbm,
    pattern,
    tip_c,
    tip_rhs,
    out,
    tip_out,
    rhs_v,
    raw,
    w_high,
    w_low,
    cur,
    sol,
    send,
    recv,
    tip_acc,
    tip_in,
    tip_sum,
    tip_all,
    in_sem,
    rhs_sem,
    cur_s,
    cur_r,
    sol_s,
    sol_r,
    row_s,
    row_r,
    tip_s1,
    tip_r1,
    tip_s2,
    tip_r2,
):
    levels, T, C, block, m, R, F, tiles_all, H = dims
    tiles_here = m * tiles_all // block
    tile = block // tiles_all
    part = R // H
    N = T * C
    row = lax.axis_index("tm")
    col = lax.axis_index("col")
    me = row * C + col
    groups = F // ROWS
    blocks = part // LANES
    G = groups * blocks * H

    sources = (inv_hbm, low_hbm, up_hbm)

    def load(level, kind):
        return pltpu.make_async_copy(
            sources[kind].at[level, 0], raw.at[level, kind], in_sem.at[level, kind]
        )

    rhs_copy = pltpu.make_async_copy(rhs_hbm.at[0], rhs_v, rhs_sem)
    rhs_copy.start()
    for level in range(levels):
        for kind in range(3):
            load(level, kind).start()

    barrier = pltpu.get_barrier_semaphore()

    @pl.loop(1, N)
    def _(k):
        other = lax.rem(me + k, N)
        pl.semaphore_signal(
            barrier,
            inc=1,
            device_id={"tm": other // C, "col": lax.rem(other, C)},
            device_id_type=MESH,
        )

    rhs_copy.wait()
    cur[0, col] = rhs_v[...].T

    def split(level, kind):
        load(level, kind).wait()

        @pl.loop(0, tiles_all)
        def _(r):
            rows = pl.ds(pl.multiple_of(r * tile, tile), tile)
            for c in range(tiles_here):
                cols = pl.ds(c * tile, tile)
                w = raw[level, kind, rows, cols]
                if kind:
                    at = ((level * 2 + kind - 1) * tiles_all + r) * tiles_here + c
                    w = w * pattern[at]
                high, low = halves_of(w)
                w_high[level, kind, rows, cols] = high
                w_low[level, kind, rows, cols] = low

    def rows_of(h):
        return pl.ds(h * part, part)

    def col_copy(buf, sems_s, sems_r, level, h, k, owner, target):
        return pltpu.make_async_remote_copy(
            src_ref=buf.at[level, owner, rows_of(h)],
            dst_ref=buf.at[level, owner, rows_of(h)],
            send_sem=sems_s.at[level, h, k - 1],
            recv_sem=sems_r.at[level, h, k - 1],
            device_id={"tm": row, "col": target},
            device_id_type=MESH,
        )

    def share(buf, sems_s, sems_r, level, h):
        for k in range(1, C):
            col_copy(buf, sems_s, sems_r, level, h, k, col, lax.rem(col + k, C)).start()

    def arrived(buf, sems_s, sems_r, level, h, k):
        owner = lax.rem(col + C - k, C)
        col_copy(buf, sems_s, sems_r, level, h, k, owner, owner).wait_recv()

    def row_copy(level, h, way):
        stride = 2**level
        target = lax.rem(row + (T - stride if way == 0 else stride), T)
        return pltpu.make_async_remote_copy(
            src_ref=send.at[level, way, rows_of(h)],
            dst_ref=recv.at[level, way, rows_of(h)],
            send_sem=row_s.at[level, h, way],
            recv_sem=row_r.at[level, h, way],
            device_id={"tm": target, "col": col},
            device_id_type=MESH,
        )

    def term(buf, level, h, k, kinds, totals):
        owner = lax.rem(col + C - k, C)
        high, low = halves_of(buf[level, owner, rows_of(h)])
        stacked = jnp.concatenate([high, low], axis=0)
        rows = pl.ds(pl.multiple_of(owner * m, m), m)
        results = []
        for kind, total in zip(kinds, totals):
            value = product(stacked, high, w_high[level, kind, rows], w_low[level, kind, rows])
            results.append(value if total is None else total + value)
        return results

    def owner_of(t):
        return (t * N) // G

    def tip_copy1(t):
        owner = owner_of(t)
        slot = lax.rem(me - owner + N, N) - 1
        return pltpu.make_async_remote_copy(
            src_ref=tip_acc.at[t],
            dst_ref=tip_in.at[slot],
            send_sem=tip_s1.at[t],
            recv_sem=tip_r1,
            device_id={"tm": owner // C, "col": lax.rem(owner, C)},
            device_id_type=MESH,
        )

    def tip_copy2(k, t):
        other = lax.rem(me + k, N)
        return pltpu.make_async_remote_copy(
            src_ref=tip_sum,
            dst_ref=tip_all.at[t],
            send_sem=tip_s2.at[k - 1],
            recv_sem=tip_r2.at[t],
            device_id={"tm": other // C, "col": lax.rem(other, C)},
            device_id_type=MESH,
        )

    def each_tile(action):
        @pl.loop(0, G)
        def _(t):
            @pl.when(owner_of(t) != me)
            def _():
                action(t)

    def each_owned(action):
        @pl.loop(0, G)
        def _(t):
            @pl.when(owner_of(t) == me)
            def _():
                action(t)

    def each_other(action):
        @pl.loop(1, N)
        def _(k):
            action(k)

    def add_tip(level, h):
        high, low = halves_of(sol[level, col, rows_of(h)])
        t_high, t_low = halves_of(tip_c[level, 0])
        nt = (((1,), (1,)), ((), ()))
        dot = functools.partial(lax.dot_general, preferred_element_type=jnp.float32)
        value = dot(t_high, high, nt) + dot(t_high, low, nt) + dot(t_low, high, nt)
        for b in range(blocks):
            piece = value[:, b * LANES : (b + 1) * LANES].reshape(groups, ROWS, LANES)
            at = pl.ds((h * blocks + b) * groups, groups)
            if level == 0:
                tip_acc[at] = piece
            else:
                tip_acc[at] = tip_acc[at] + piece

    def settled(level, h):
        row_copy(level, h, 0).wait_recv()
        row_copy(level, h, 1).wait_recv()
        return (
            cur[level, col, rows_of(h)] - recv[level, 0, rows_of(h)] - recv[level, 1, rows_of(h)]
        )

    pl.semaphore_wait(barrier, N - 1)
    for h in range(H):
        share(cur, cur_s, cur_r, 0, h)
    split(0, 0)

    for level in range(levels):
        for h in range(H):
            if level:
                cur[level, col, rows_of(h)] = settled(level - 1, h)
                share(cur, cur_s, cur_r, level, h)
            total = [None]
            for k in range(C):
                if k:
                    arrived(cur, cur_s, cur_r, level, h, k)
                total = term(cur, level, h, k, (0,), total)
            sol[level, col, rows_of(h)] = total[0]
            share(sol, sol_s, sol_r, level, h)
            add_tip(level, h)
            if level == levels - 1 and h == H - 1:
                each_tile(lambda t: tip_copy1(t).start())
            if level == 0 and h == 0:
                split(0, 1)
                split(0, 2)
            totals = [None, None]
            for k in range(C - 1):
                if k:
                    arrived(sol, sol_s, sol_r, level, h, k)
                totals = term(sol, level, h, k, (1, 2), totals)
            k = C - 1
            if k:
                arrived(sol, sol_s, sol_r, level, h, k)
            for way in range(2):
                send[level, way, rows_of(h)] = term(sol, level, h, k, (1 + way,), totals[way : way + 1])[0]
                row_copy(level, h, way).start()
        if level < levels - 1:
            for kind in range(3):
                split(level + 1, kind)

    def reduce_mine(t):
        pltpu.make_async_copy(tip_in, tip_in, tip_r1).wait()
        tip_sum[...] = tip_acc[t] + jnp.sum(tip_in[...], axis=0)
        tip_all[t] = tip_sum[...]
        each_other(lambda k: tip_copy2(k, t).start())

    each_owned(reduce_mine)
    for h in range(H):
        out[0, :, h * part : (h + 1) * part] = settled(levels - 1, h).T
    each_tile(lambda t: tip_copy2(1, t).wait_recv())
    for h in range(H):
        for b in range(blocks):
            at = h * blocks + b
            lanes = slice(at * LANES, (at + 1) * LANES)
            total = tip_all[at * groups : (at + 1) * groups].reshape(F, LANES)
            tip_out[:, lanes] = tip_rhs[:, lanes] - total

    for level in range(levels):
        for h in range(H):
            for k in range(1, C):
                target = lax.rem(col + k, C)
                col_copy(cur, cur_s, cur_r, level, h, k, col, target).wait_send()
                col_copy(sol, sol_s, sol_r, level, h, k, col, target).wait_send()
            for way in range(2):
                row_copy(level, h, way).wait_send()
    each_tile(lambda t: tip_copy1(t).wait_send())
    each_owned(lambda t: each_other(lambda k: tip_copy2(k, t).wait_send()))


HALVES = 2


def solution(mesh):
    T, C = mesh.shape["tm"], mesh.shape["col"]

    def local(rhs, inverse, lower, upper, tile_pattern, tip_coupling, tip_rhs):
        levels, _, block, m = inverse.shape
        R = rhs.shape[2]
        F = tip_rhs.shape[0]
        H = HALVES
        dims = (levels, T, C, block, m, R, F, tile_pattern.shape[3], H)
        N = T * C
        G = (F // ROWS) * (R // LANES)
        f32, b16 = jnp.float32, jnp.bfloat16
        dma = pltpu.SemaphoreType.DMA
        peers = max(C - 1, 1)
        anywhere = pl.BlockSpec(memory_space=pl.ANY)
        vmem = pl.BlockSpec(memory_space=pltpu.VMEM)
        return pl.pallas_call(
            functools.partial(kernel, dims),
            out_shape=(
                jax.ShapeDtypeStruct((1, m, R), f32),
                jax.ShapeDtypeStruct((F, R), f32),
            ),
            in_specs=[anywhere] * 4 + [pl.BlockSpec(memory_space=pltpu.SMEM), vmem, vmem],
            out_specs=(vmem, vmem),
            scratch_shapes=[
                pltpu.VMEM((m, R), f32),
                pltpu.VMEM((levels, 3, block, m), f32),
                pltpu.VMEM((levels, 3, block, m), b16),
                pltpu.VMEM((levels, 3, block, m), b16),
                pltpu.VMEM((levels, C, R, m), f32),
                pltpu.VMEM((levels, C, R, m), f32),
                pltpu.VMEM((levels, 2, R, m), f32),
                pltpu.VMEM((levels, 2, R, m), f32),
                pltpu.VMEM((G, ROWS, LANES), f32),
                pltpu.VMEM((N - 1, ROWS, LANES), f32),
                pltpu.VMEM((ROWS, LANES), f32),
                pltpu.VMEM((G, ROWS, LANES), f32),
                dma((levels, 3)),
                dma,
                dma((levels, H, peers)),
                dma((levels, H, peers)),
                dma((levels, H, peers)),
                dma((levels, H, peers)),
                dma((levels, H, 2)),
                dma((levels, H, 2)),
                dma((G,)),
                dma,
                dma((N - 1,)),
                dma((G,)),
            ],
            compiler_params=pltpu.CompilerParams(
                collective_id=0, has_side_effects=True, vmem_limit_bytes=60 * 2**20
            ),
        )(
            rhs,
            inverse,
            lower,
            upper,
            tile_pattern.astype(f32).reshape(-1),
            tip_coupling,
            tip_rhs,
        )

    return jax.shard_map(
        local,
        mesh=mesh,
        in_specs=(
            P("tm", "col", None),
            P(None, "tm", None, "col"),
            P(None, "tm", None, "col"),
            P(None, "tm", None, "col"),
            P(None, "tm", None, None, "col"),
            P(None, "tm", None, "col"),
            P(),
        ),
        out_specs=(P("tm", "col", None), P()),
        check_vma=False,
    )
```

```python
import functools

import jax
import jax.numpy as jnp
from jax import lax
from jax.experimental import pallas as pl
from jax.experimental.pallas import tpu as pltpu
from jax.sharding import PartitionSpec as P

MESH = pl.DeviceIdType.MESH
LANES = 128
ROWS = 8


def halves_of(x):
    high = x.astype(jnp.bfloat16)
    low = (x - high.astype(jnp.float32)).astype(jnp.bfloat16)
    return high, low


def product(stacked, high, w_high, w_low):
    rows = high.shape[0]
    both = jnp.dot(stacked, w_high, preferred_element_type=jnp.float32)
    return both[:rows] + both[rows:] + jnp.dot(high, w_low, preferred_element_type=jnp.float32)


def kernel(
    dims,
    rhs_hbm,
    inv_hbm,
    low_hbm,
    up_hbm,
    pattern,
    tip_c,
    tip_rhs,
    out,
    tip_out,
    rhs_v,
    raw,
    w_high,
    w_low,
    cur,
    sol,
    send,
    recv,
    joined,
    tip_acc,
    tip_in,
    tip_sum,
    tip_all,
    in_sem,
    rhs_sem,
    cur_s,
    cur_r,
    sol_s,
    sol_r,
    row_s,
    row_r,
    tip_s1,
    tip_r1,
    tip_s2,
    tip_r2,
):
    levels, T, C, block, m, R, F, tiles_all, H = dims
    tiles_here = m * tiles_all // block
    tile = block // tiles_all
    part = R // H
    N = T * C
    row = lax.axis_index("tm")
    col = lax.axis_index("col")
    me = row * C + col
    groups = F // ROWS
    blocks = part // LANES
    G = groups * blocks * H

    sources = (inv_hbm, low_hbm, up_hbm)

    def load(level, kind):
        return pltpu.make_async_copy(
            sources[kind].at[level, 0], raw.at[level, kind], in_sem.at[level, kind]
        )

    rhs_copy = pltpu.make_async_copy(rhs_hbm.at[0], rhs_v, rhs_sem)
    rhs_copy.start()
    for level in range(levels):
        for kind in range(3):
            load(level, kind).start()

    barrier = pltpu.get_barrier_semaphore()

    @pl.loop(1, N)
    def _(k):
        other = lax.rem(me + k, N)
        pl.semaphore_signal(
            barrier,
            inc=1,
            device_id={"tm": other // C, "col": lax.rem(other, C)},
            device_id_type=MESH,
        )

    rhs_copy.wait()
    cur[0, col] = rhs_v[...].T

    def split(level, kind):
        load(level, kind).wait()

        @pl.loop(0, tiles_all)
        def _(r):
            rows = pl.ds(pl.multiple_of(r * tile, tile), tile)
            for c in range(tiles_here):
                cols = pl.ds(c * tile, tile)
                w = raw[level, kind, rows, cols]
                if kind:
                    at = ((level * 2 + kind - 1) * tiles_all + r) * tiles_here + c
                    w = w * pattern[at]
                high, low = halves_of(w)
                w_high[level, kind, rows, cols] = high
                w_low[level, kind, rows, cols] = low

    def rows_of(h):
        return pl.ds(h * part, part)

    def col_copy(buf, sems_s, sems_r, level, h, k, owner, target):
        return pltpu.make_async_remote_copy(
            src_ref=buf.at[level, owner, rows_of(h)],
            dst_ref=buf.at[level, owner, rows_of(h)],
            send_sem=sems_s.at[level, h, k - 1],
            recv_sem=sems_r.at[level, h, k - 1],
            device_id={"tm": row, "col": target},
            device_id_type=MESH,
        )

    def share(buf, sems_s, sems_r, level, h):
        for k in range(1, C):
            col_copy(buf, sems_s, sems_r, level, h, k, col, lax.rem(col + k, C)).start()

    def arrived(buf, sems_s, sems_r, level, h, k):
        owner = lax.rem(col + C - k, C)
        col_copy(buf, sems_s, sems_r, level, h, k, owner, owner).wait_recv()

    def bit_of(level):
        return lax.rem(row // 2**level, 2)

    def row_copy(level, h, way):
        stride = 2**level
        if level == levels - 1:
            target = lax.rem(row + (T - stride if way == 0 else stride), T)
            source = send.at[level, way, rows_of(h)]
        elif way == 0:
            target = lax.rem(row + T - 2 * stride + 4 * stride * bit_of(level), T)
            source = send.at[level, bit_of(level), rows_of(h)]
        else:
            target = row + stride - 2 * stride * bit_of(level)
            source = joined.at[level, rows_of(h)]
        return pltpu.make_async_remote_copy(
            src_ref=source,
            dst_ref=recv.at[level, way, rows_of(h)],
            send_sem=row_s.at[level, h, way],
            recv_sem=row_r.at[level, h, way],
            device_id={"tm": target, "col": col},
            device_id_type=MESH,
        )

    def join(level, h):
        row_copy(level, h, 0).wait_recv()
        joined[level, rows_of(h)] = (
            send[level, 1 - bit_of(level), rows_of(h)] + recv[level, 0, rows_of(h)]
        )
        row_copy(level, h, 1).start()

    def term(buf, level, h, k, kinds, totals):
        owner = lax.rem(col + C - k, C)
        high, low = halves_of(buf[level, owner, rows_of(h)])
        stacked = jnp.concatenate([high, low], axis=0)
        rows = pl.ds(pl.multiple_of(owner * m, m), m)
        results = []
        for kind, total in zip(kinds, totals):
            value = product(stacked, high, w_high[level, kind, rows], w_low[level, kind, rows])
            results.append(value if total is None else total + value)
        return results

    def owner_of(t):
        return (t * N) // G

    def tip_copy1(t):
        owner = owner_of(t)
        slot = lax.rem(me - owner + N, N) - 1
        return pltpu.make_async_remote_copy(
            src_ref=tip_acc.at[t],
            dst_ref=tip_in.at[slot],
            send_sem=tip_s1.at[t],
            recv_sem=tip_r1,
            device_id={"tm": owner // C, "col": lax.rem(owner, C)},
            device_id_type=MESH,
        )

    def tip_copy2(k, t):
        other = lax.rem(me + k, N)
        return pltpu.make_async_remote_copy(
            src_ref=tip_sum,
            dst_ref=tip_all.at[t],
            send_sem=tip_s2.at[k - 1],
            recv_sem=tip_r2.at[t],
            device_id={"tm": other // C, "col": lax.rem(other, C)},
            device_id_type=MESH,
        )

    def each_tile(action):
        @pl.loop(0, G)
        def _(t):
            @pl.when(owner_of(t) != me)
            def _():
                action(t)

    def each_owned(action):
        @pl.loop(0, G)
        def _(t):
            @pl.when(owner_of(t) == me)
            def _():
                action(t)

    def each_other(action):
        @pl.loop(1, N)
        def _(k):
            action(k)

    def add_tip(level, h):
        high, low = halves_of(sol[level, col, rows_of(h)])
        t_high, t_low = halves_of(tip_c[level, 0])
        nt = (((1,), (1,)), ((), ()))
        dot = functools.partial(lax.dot_general, preferred_element_type=jnp.float32)
        value = dot(t_high, high, nt) + dot(t_high, low, nt) + dot(t_low, high, nt)
        for b in range(blocks):
            piece = value[:, b * LANES : (b + 1) * LANES].reshape(groups, ROWS, LANES)
            at = pl.ds((h * blocks + b) * groups, groups)
            if level == 0:
                tip_acc[at] = piece
            else:
                tip_acc[at] = tip_acc[at] + piece

    def settled(level, h):
        row_copy(level, h, 1).wait_recv()
        value = cur[level, col, rows_of(h)] - recv[level, 1, rows_of(h)]
        if level == levels - 1:
            row_copy(level, h, 0).wait_recv()
            value = value - recv[level, 0, rows_of(h)]
        return value

    for kind in range(3):
        split(0, kind)
    pl.semaphore_wait(barrier, N - 1)
    for h in range(H):
        share(cur, cur_s, cur_r, 0, h)

    for level in range(levels):
        for h in range(H):
            if level:
                cur[level, col, rows_of(h)] = settled(level - 1, h)
                share(cur, cur_s, cur_r, level, h)
            total = [None]
            for k in range(C):
                if k:
                    arrived(cur, cur_s, cur_r, level, h, k)
                total = term(cur, level, h, k, (0,), total)
            sol[level, col, rows_of(h)] = total[0]
            share(sol, sol_s, sol_r, level, h)
            add_tip(level, h)
            if level == levels - 1 and h == H - 1:
                each_tile(lambda t: tip_copy1(t).start())
            if level < levels - 1:
                ways = (bit_of(level), 1 - bit_of(level))
            else:
                ways = (0, 1)
            kinds = (1 + ways[0], 1 + ways[1])
            totals = [None, None]
            for k in range(C - 1):
                if k:
                    arrived(sol, sol_s, sol_r, level, h, k)
                totals = term(sol, level, h, k, kinds, totals)
            k = C - 1
            if k:
                arrived(sol, sol_s, sol_r, level, h, k)
            for i in range(2):
                value = term(sol, level, h, k, kinds[i : i + 1], totals[i : i + 1])[0]
                send[level, ways[i], rows_of(h)] = value
                if i == 0 or level == levels - 1:
                    row_copy(level, h, i).start()
        if level < levels - 1:
            for h in range(H):
                join(level, h)
            for kind in range(3):
                split(level + 1, kind)

    def reduce_mine(t):
        pltpu.make_async_copy(tip_in, tip_in, tip_r1).wait()
        tip_sum[...] = tip_acc[t] + jnp.sum(tip_in[...], axis=0)
        tip_all[t] = tip_sum[...]
        each_other(lambda k: tip_copy2(k, t).start())

    each_owned(reduce_mine)
    for h in range(H):
        out[0, :, h * part : (h + 1) * part] = settled(levels - 1, h).T
    each_tile(lambda t: tip_copy2(1, t).wait_recv())
    for h in range(H):
        for b in range(blocks):
            at = h * blocks + b
            lanes = slice(at * LANES, (at + 1) * LANES)
            total = tip_all[at * groups : (at + 1) * groups].reshape(F, LANES)
            tip_out[:, lanes] = tip_rhs[:, lanes] - total

    for level in range(levels):
        for h in range(H):
            for k in range(1, C):
                target = lax.rem(col + k, C)
                col_copy(cur, cur_s, cur_r, level, h, k, col, target).wait_send()
                col_copy(sol, sol_s, sol_r, level, h, k, col, target).wait_send()
            for way in range(2):
                row_copy(level, h, way).wait_send()
    each_tile(lambda t: tip_copy1(t).wait_send())
    each_owned(lambda t: each_other(lambda k: tip_copy2(k, t).wait_send()))


HALVES = 2


def solution(mesh):
    T, C = mesh.shape["tm"], mesh.shape["col"]

    def local(rhs, inverse, lower, upper, tile_pattern, tip_coupling, tip_rhs):
        levels, _, block, m = inverse.shape
        R = rhs.shape[2]
        F = tip_rhs.shape[0]
        H = HALVES
        dims = (levels, T, C, block, m, R, F, tile_pattern.shape[3], H)
        N = T * C
        G = (F // ROWS) * (R // LANES)
        f32, b16 = jnp.float32, jnp.bfloat16
        dma = pltpu.SemaphoreType.DMA
        peers = max(C - 1, 1)
        anywhere = pl.BlockSpec(memory_space=pl.ANY)
        vmem = pl.BlockSpec(memory_space=pltpu.VMEM)
        return pl.pallas_call(
            functools.partial(kernel, dims),
            out_shape=(
                jax.ShapeDtypeStruct((1, m, R), f32),
                jax.ShapeDtypeStruct((F, R), f32),
            ),
            in_specs=[anywhere] * 4 + [pl.BlockSpec(memory_space=pltpu.SMEM), vmem, vmem],
            out_specs=(vmem, vmem),
            scratch_shapes=[
                pltpu.VMEM((m, R), f32),
                pltpu.VMEM((levels, 3, block, m), f32),
                pltpu.VMEM((levels, 3, block, m), b16),
                pltpu.VMEM((levels, 3, block, m), b16),
                pltpu.VMEM((levels, C, R, m), f32),
                pltpu.VMEM((levels, C, R, m), f32),
                pltpu.VMEM((levels, 2, R, m), f32),
                pltpu.VMEM((levels, 2, R, m), f32),
                pltpu.VMEM((max(levels - 1, 1), R, m), f32),
                pltpu.VMEM((G, ROWS, LANES), f32),
                pltpu.VMEM((N - 1, ROWS, LANES), f32),
                pltpu.VMEM((ROWS, LANES), f32),
                pltpu.VMEM((G, ROWS, LANES), f32),
                dma((levels, 3)),
                dma,
                dma((levels, H, peers)),
                dma((levels, H, peers)),
                dma((levels, H, peers)),
                dma((levels, H, peers)),
                dma((levels, H, 2)),
                dma((levels, H, 2)),
                dma((G,)),
                dma,
                dma((N - 1,)),
                dma((G,)),
            ],
            compiler_params=pltpu.CompilerParams(
                collective_id=0, has_side_effects=True, vmem_limit_bytes=60 * 2**20
            ),
        )(
            rhs,
            inverse,
            lower,
            upper,
            tile_pattern.astype(f32).reshape(-1),
            tip_coupling,
            tip_rhs,
        )

    return jax.shard_map(
        local,
        mesh=mesh,
        in_specs=(
            P("tm", "col", None),
            P(None, "tm", None, "col"),
            P(None, "tm", None, "col"),
            P(None, "tm", None, "col"),
            P(None, "tm", None, None, "col"),
            P(None, "tm", None, "col"),
            P(),
        ),
        out_specs=(P("tm", "col", None), P()),
        check_vma=False,
    )
```
